256 devices in a mesh: row: 32 (over z, x), feat: 8 (over y, core).
Axes of the slice: x: 4, y: 4, z: 8, core: 2. Of those that a mesh axis runs over, the one named last changes fastest.
Arguments:
- bin_codes: int32 [256, 262144], P(None, 'row'), may hold values from 0 to 31
- gradients: bfloat16 [262144], P('row'), may hold values from -6 to 6
- hessians: bfloat16 [262144], P('row'), may hold values from 0.019897461 to 0.25
- pair_list: int32 [64, 2], replicated, may hold values from 0 to 255, as said below
- owners: int32 [64], replicated, may hold values from 0 to 7, as said below
Outputs:
- cut_table: float32 [128, 1024], P('feat', 'row')
- best_gain: float32 [64], replicated
The draws below stay inside these ranges and needn't reach their ends.
Inputs may be any that keep to these rules, and one draw needn't show every extreme that they name: `pair_list`: each row holds two different features, the first smaller. `owners`: one index owns exactly 16 pairs in every draw, the others at most that many.
All inputs are finite; a program needn't handle non-finite values.
Results may differ from the reference program's by a relative error of at most 0.0003.
Values sent between devices are 32-bit elements; how exact they have to be, the bound alone decides.
A program may use at most 64 MiB of HBM per device.

```python
import math
import jax
import jax.numpy as jnp
from jax import lax

F = 256
BINS = 32
P_SIZE = 64
ROWS = 262144
SLOTS = 16
N_FEAT = 8


def draw_pair_list(key, part):
    first_key = jax.random.fold_in(key, 11)
    step_key = jax.random.fold_in(key, 12)
    first = jax.random.randint(first_key, (P_SIZE,), 0, F, dtype=jnp.int32)
    offset = jax.random.randint(step_key, (P_SIZE,), 1, F, dtype=jnp.int32)
    second = (first + offset) % F
    return jnp.stack([jnp.minimum(first, second), jnp.maximum(first, second)], axis=1).astype(jnp.int32)


def draw_owners(key, part):
    order_key = jax.random.fold_in(key, 21)
    heavy_key = jax.random.fold_in(key, 22)
    order = jax.random.permutation(order_key, P_SIZE).astype(jnp.int32)
    heavy = jax.random.randint(heavy_key, (), 0, N_FEAT, dtype=jnp.int32)
    places = jnp.arange(P_SIZE, dtype=jnp.int32)
    others = (heavy + 1 + (places - SLOTS) % (N_FEAT - 1)) % N_FEAT
    assigned = jnp.where(places < SLOTS, heavy, others).astype(jnp.int32)
    inverse = jnp.argsort(order, stable=True)
    return assigned[inverse].astype(jnp.int32)


def plant(values, rng, low, high):
    shape = values.shape
    index_at = [jax.random.randint(jax.random.fold_in(rng, axis), (), 0, shape[axis]) for axis in range(len(shape))]
    values = values.at[tuple(index_at)].set(low)
    longest = shape.index(max(shape))
    index_at[longest] = (index_at[longest] + 1) % shape[longest]
    return values.at[tuple(index_at)].set(high)


def steps_of(stream_key, dims, shards, low, largest):
    def one(dim, shards_of):
        draws = jax.random.uniform(jax.random.fold_in(jax.random.fold_in(stream_key, 6), dim), (shards_of,), jnp.float32, low / len(shards), largest / len(shards))
        return jnp.repeat(jnp.exp(draws), dims[dim] // shards_of).reshape((-1,) + (1,) * (len(dims) - dim - 1))

    level = one(*shards[0])
    for cut in shards[1:]:
        level = level * one(*cut)
    return level


def centred(key, shape, spread, reach, shards=(), kind=jnp.bfloat16):
    array = jax.random.normal(key, shape, jnp.float32) * spread
    if len(shards) > 0:
        array = steps_of(key, shape, shards, -0.22, 0.18) * array
    return jnp.clip(array, min=-reach, max=reach).astype(kind)


def setup_inputs(seed: int = 0) -> dict:
    streams_of = jax.random.split(jax.random.key(seed), 6)
    return {
        "bin_codes": plant(jax.random.randint(streams_of[0], (F, ROWS), 0, BINS), jax.random.fold_in(streams_of[0], 1), 0, BINS - 1).astype(jnp.int32),
        "gradients": centred(streams_of[1], (ROWS,), 1.0, 6.0, ((0, 32),)),
        "hessians": jnp.clip(jnp.exp(math.log(0.25) - 2.5308688 * jax.random.uniform(streams_of[2], (ROWS,), jnp.float32) ** steps_of(streams_of[2], (ROWS,), ((0, 32),), -0.2, 0.2)), 0.019897461, 0.25).astype(jnp.bfloat16),
        "pair_list": draw_pair_list(jax.random.fold_in(streams_of[5], 71), 0),
        "owners": draw_owners(jax.random.fold_in(streams_of[5], 71), 0),
    }


LAMBDA_REG = 1.0


def slot_rank(owners):
    pair_ids = jnp.arange(owners.shape[0], dtype=jnp.int32)
    same_owner = owners[:, None] == owners[None, :]
    earlier = pair_ids[None, :] < pair_ids[:, None]
    return jnp.sum((same_owner & earlier).astype(jnp.int32), axis=1)


def cumulate(histogram):
    bin_count = histogram.shape[-2]
    running = jnp.cumsum(histogram, axis=-2)
    shaped = running.reshape(running.shape[:-1] + (2, bin_count))
    shaped = jnp.cumsum(shaped, axis=-1)
    return shaped.reshape(running.shape)


def cut_gains(cut_rows, margin_row):
    bin_count = margin_row.shape[-1] // 2
    grad_cum = cut_rows[..., :bin_count]
    hess_cum = cut_rows[..., bin_count:]
    grad_end = grad_cum[..., -1:]
    hess_end = hess_cum[..., -1:]
    grad_col = margin_row[..., None, :bin_count]
    hess_col = margin_row[..., None, bin_count:]
    grad_all = margin_row[..., None, bin_count - 1:bin_count]
    hess_all = margin_row[..., None, 2 * bin_count - 1:]
    quad_grad = (grad_cum, grad_end - grad_cum, grad_col - grad_cum, grad_all - grad_end - grad_col + grad_cum)
    quad_hess = (hess_cum, hess_end - hess_cum, hess_col - hess_cum, hess_all - hess_end - hess_col + hess_cum)
    result = -(grad_all * grad_all) / (hess_all + LAMBDA_REG)
    for grad_part, hess_part in zip(quad_grad, quad_hess):
        result = result + grad_part * grad_part / (hess_part + LAMBDA_REG)
    return result


def pair_histogram(bin_codes, gradients, hessians, pair_row):
    levels = jnp.arange(BINS, dtype=jnp.int32)
    first_col = lax.dynamic_index_in_dim(bin_codes, pair_row[0], 0, keepdims=False)
    second_col = lax.dynamic_index_in_dim(bin_codes, pair_row[1], 0, keepdims=False)
    hot_first = (first_col[:, None] == levels[None, :]).astype(jnp.float32)
    hot_second = (second_col[:, None] == levels[None, :]).astype(jnp.float32)
    weighted = jnp.concatenate([hot_second * gradients.astype(jnp.float32)[:, None], hot_second * hessians.astype(jnp.float32)[:, None]], axis=1)
    return jnp.dot(hot_first.T, weighted, precision=lax.Precision.HIGHEST, preferred_element_type=jnp.float32)


def reference(bin_codes, gradients, hessians, pair_list, owners):
    histogram = lax.map(lambda pair_row: pair_histogram(bin_codes, gradients, hessians, pair_row), pair_list)
    running = cumulate(histogram)
    cut_gain = cut_gains(running, running[:, -1, :]).reshape(P_SIZE, BINS * BINS)
    best_gain = jnp.max(cut_gain, axis=1)
    rank = slot_rank(owners)
    table_ids = jnp.arange(N_FEAT * SLOTS, dtype=jnp.int32)
    owner_of = table_ids // SLOTS
    place_of = table_ids % SLOTS
    matched = (owners[None, :] == owner_of[:, None]) & (rank[None, :] == place_of[:, None])
    pair_ids = jnp.arange(P_SIZE, dtype=jnp.int32)
    chosen = jnp.sum(jnp.where(matched, pair_ids[None, :], 0), axis=1).astype(jnp.int32)
    has_pair = jnp.any(matched, axis=1)
    cut_table = jnp.where(has_pair[:, None], cut_gain[chosen], jnp.float32(0.0))
    return cut_table, best_gain
```

```python
import jax
import jax.numpy as jnp
from jax import lax
from jax.experimental import pallas as pl
from jax.experimental.pallas import tpu as pltpu
from jax.sharding import PartitionSpec as P

BINS = 32
LAMBDA_REG = 1.0
ROW = 32
FEAT = 8
PAIRS = 8
CHUNKS = 4
STEP = 1024
MESH = pl.DeviceIdType.MESH


def kernel(pairs_ref, owners_ref, grad_ref, hess_ref, codes_hbm, table_ref, best_ref,
           codes_0, codes_1, codes_2, codes_3, acc, send, recv, gains, peak, peaks,
           code_sem, sum_send, sum_recv, gain_send, gain_recv, peak_send, peak_recv):
    row = lax.axis_index("row")
    feat = lax.axis_index("feat")
    chunks = (codes_0, codes_1, codes_2, codes_3)
    chunk_width = codes_0.shape[1]
    width = STEP

    def fetch(c):
        lanes = pl.ds(c * chunk_width, chunk_width)
        return pltpu.make_async_copy(codes_hbm.at[:, lanes], chunks[c], code_sem.at[c])

    for c in range(CHUNKS):
        fetch(c).start()

    barrier = pltpu.get_barrier_semaphore()

    @pl.loop(1, ROW)
    def _(k):
        other = lax.rem(row + k, ROW)
        pl.semaphore_signal(barrier, inc=1, device_id=(other, feat), device_id_type=MESH)

    @pl.loop(1, FEAT)
    def _(k):
        other = lax.rem(feat + k, FEAT)
        pl.semaphore_signal(barrier, inc=1, device_id=(row, other), device_id_type=MESH)

    acc[...] = jnp.zeros_like(acc)
    level = lax.broadcasted_iota(jnp.int32, (16, width), 0).astype(jnp.float32).astype(jnp.bfloat16)
    level_up = level + jnp.bfloat16(16)
    one = jnp.ones((16, width), jnp.bfloat16)
    zero = jnp.zeros((16, width), jnp.bfloat16)
    sub = width // 128

    def accumulate(c, codes, inner):
        start = pl.multiple_of(inner * width, width)
        block = c * (chunk_width // width) + inner

        def spread(ref):
            rows = ref[pl.ds(pl.multiple_of(block * sub, sub), sub), :].astype(jnp.float32)
            flat = jnp.concatenate([rows[j:j + 1, :] for j in range(sub)], axis=1)
            return jnp.broadcast_to(flat, (16, width)).astype(jnp.bfloat16)

        grad = spread(grad_ref)
        hess = spread(hess_ref)
        for group in range(2):
            first, second = [], []
            for i in range(4):
                p = feat * PAIRS + group * 4 + i
                ca = codes[pl.ds(pairs_ref[0, p], 1), pl.ds(start, width)].astype(jnp.float32)
                cb = codes[pl.ds(pairs_ref[1, p], 1), pl.ds(start, width)].astype(jnp.float32)
                ca = jnp.broadcast_to(ca, (16, width)).astype(jnp.bfloat16)
                cb = jnp.broadcast_to(cb, (16, width)).astype(jnp.bfloat16)
                first += [jnp.where(ca <= level, one, zero), jnp.where(ca <= level_up, one, zero)]
                low, high = cb <= level, cb <= level_up
                second += [jnp.where(low, grad, zero), jnp.where(high, grad, zero),
                           jnp.where(low, hess, zero), jnp.where(high, hess, zero)]
            lhs = jnp.concatenate(first, axis=0)
            rhs = jnp.concatenate(second, axis=0)
            acc[group] += lax.dot_general(lhs, rhs, (((1,), (1,)), ((), ())),
                                          preferred_element_type=jnp.float32)

    for c in range(CHUNKS):
        fetch(c).wait()

        @pl.loop(0, chunk_width // width)
        def _(inner):
            accumulate(c, chunks[c], inner)

    for p in range(PAIRS):
        group, i = p // 4, p % 4
        block = acc[group, 32 * i:32 * i + 32, 64 * i:64 * i + 64]
        last = jnp.broadcast_to(block[31:32, :], (BINS, 64))
        send[:, p, :] = jnp.concatenate([block, last], axis=1)

    mine = owners_ref[...] == feat
    mine_value = jnp.where(mine, 1.0, 0.0).astype(jnp.bfloat16)
    before = lax.broadcasted_iota(jnp.int32, (64, 64), 0) < lax.broadcasted_iota(jnp.int32, (64, 64), 1)
    rank = jnp.dot(mine_value, jnp.where(before, 1.0, 0.0).astype(jnp.bfloat16),
                   preferred_element_type=jnp.float32)
    slot = lax.broadcasted_iota(jnp.int32, (16, 64), 0).astype(jnp.float32)
    chosen = jnp.where((jnp.broadcast_to(rank, (16, 64)) == slot) & jnp.broadcast_to(mine, (16, 64)), 1.0, 0.0)

    pl.semaphore_wait(barrier, ROW - 1 + FEAT - 1)

    @pl.loop(1, ROW)
    def _(k):
        other = lax.rem(row + k, ROW)
        pltpu.make_async_remote_copy(
            src_ref=send.at[other], dst_ref=recv.at[row], send_sem=sum_send, recv_sem=sum_recv,
            device_id=(other, feat), device_id_type=MESH).start()

    recv[row] = send[row]
    others = recv.at[pl.ds(0, ROW - 1)]
    pltpu.make_async_copy(others, others, sum_recv).wait()
    total = jnp.sum(recv[...], axis=0)

    grad_cum = total[:, 0:32]
    hess_cum = total[:, 32:64]
    grad_col = total[:, 64:96]
    hess_col = total[:, 96:128]
    grad_end = total[:, 31:32]
    hess_end = total[:, 63:64]
    grad_all = total[:, 95:96]
    hess_all = total[:, 127:128]
    quad_grad = (grad_cum, grad_end - grad_cum, grad_col - grad_cum, grad_all - grad_end - grad_col + grad_cum)
    quad_hess = (hess_cum, hess_end - hess_cum, hess_col - hess_cum, hess_all - hess_end - hess_col + hess_cum)
    gain = -(grad_all * grad_all) / (hess_all + LAMBDA_REG)
    for grad_part, hess_part in zip(quad_grad, quad_hess):
        gain = gain + grad_part * grad_part / (hess_part + LAMBDA_REG)
    tile = jnp.concatenate([gain, gain, gain, gain], axis=1)
    gains[feat] = tile

    @pl.loop(1, FEAT)
    def _(k):
        other = lax.rem(feat + k, FEAT)
        pltpu.make_async_remote_copy(
            src_ref=gains.at[feat], dst_ref=gains.at[feat], send_sem=gain_send, recv_sem=gain_recv,
            device_id=(row, other), device_id_type=MESH).start()

    others = gains.at[pl.ds(0, FEAT - 1)]
    pltpu.make_async_copy(others, others, gain_recv).wait()
    every = gains[...].reshape(FEAT * PAIRS, 128)
    top = jnp.max(every.T[0:32, :], axis=0, keepdims=True)
    top = jnp.concatenate([top, top], axis=1)
    peak[...] = top

    @pl.loop(1, ROW)
    def _(k):
        other = lax.rem(row + k, ROW)
        pltpu.make_async_remote_copy(
            src_ref=peak, dst_ref=peaks.at[row], send_sem=peak_send, recv_sem=peak_recv,
            device_id=(other, feat), device_id_type=MESH).start()

    table_ref[...] = jnp.dot(chosen, every, precision=lax.Precision.HIGHEST,
                             preferred_element_type=jnp.float32)[:, 0:32]
    peaks[row] = top
    others = peaks.at[pl.ds(0, ROW - 1)]
    pltpu.make_async_copy(others, others, peak_recv).wait()
    best_ref[...] = jnp.max(peaks[...], axis=0)[:, 0:64]

    sent = send.at[pl.ds(0, ROW - 1)]
    pltpu.make_async_copy(sent, sent, sum_send).wait()
    sent = gains.at[pl.ds(0, FEAT - 1)]
    pltpu.make_async_copy(sent, sent, gain_send).wait()
    sent = peaks.at[pl.ds(0, ROW - 1)]
    pltpu.make_async_copy(sent, sent, peak_send).wait()


def shards(bin_codes, gradients, hessians, pair_list, owners):
    rows = bin_codes.shape[1]
    vmem = pl.BlockSpec(memory_space=pltpu.VMEM)
    table, best = pl.pallas_call(
        kernel,
        out_shape=(jax.ShapeDtypeStruct((16, BINS), jnp.float32),
                   jax.ShapeDtypeStruct((1, FEAT * PAIRS), jnp.float32)),
        in_specs=[pl.BlockSpec(memory_space=pltpu.SMEM), vmem, vmem, vmem,
                  pl.BlockSpec(memory_space=pl.ANY)],
        out_specs=(vmem, vmem),
        scratch_shapes=[pltpu.VMEM((bin_codes.shape[0], rows // CHUNKS), jnp.int32)] * CHUNKS + [
            pltpu.VMEM((2, 128, 256), jnp.float32),
            pltpu.VMEM((ROW, PAIRS, 128), jnp.float32),
            pltpu.VMEM((ROW, PAIRS, 128), jnp.float32),
            pltpu.VMEM((FEAT, PAIRS, 128), jnp.float32),
            pltpu.VMEM((1, 128), jnp.float32),
            pltpu.VMEM((ROW, 1, 128), jnp.float32),
            pltpu.SemaphoreType.DMA((CHUNKS,)),
        ] + [pltpu.SemaphoreType.DMA] * 6,
        compiler_params=pltpu.CompilerParams(collective_id=0, has_side_effects=True),
    )(pair_list.T, owners.reshape(1, -1), gradients.reshape(rows // 128, 128),
      hessians.reshape(rows // 128, 128), bin_codes)
    return table, best.reshape(-1)


def solution(mesh):
    in_specs = (P(None, "row"), P("row"), P("row"), P(), P())
    out_specs = (P("feat", "row"), P())
    return jax.shard_map(shards, mesh=mesh, in_specs=in_specs, out_specs=out_specs, check_vma=False)
```

```python
import jax
import jax.numpy as jnp
from jax import lax
from jax.experimental import pallas as pl
from jax.experimental.pallas import tpu as pltpu
from jax.sharding import PartitionSpec as P

BINS = 32
LAMBDA_REG = 1.0
Z = 8
X = 4
FEAT = 8
PAIRS = 8
CHUNKS = 4
STEP = 2048
MESH = pl.DeviceIdType.MESH
Z_STEPS = (4, 3, 5, 2, 6, 1, 7)
PLANE_STEPS = sorted(
    [(dx, df) for dx in range(X) for df in range(FEAT) if (dx, df) != (0, 0)],
    key=lambda s: -(min(s[0], X - s[0]) + min(s[1], FEAT - s[1]) / 2),
)


def kernel(pairs_hbm, owners_hbm, grad_hbm, hess_hbm, codes_hbm, table_ref, best_ref,
           chunks, pairs_ref, owners_ref, grad_ref, hess_ref,
           acc, send, recv, parts, gain_ref, message, inbox,
           code_sem, small_sem, x_send, x_recv, z_send, z_recv, plane_send, plane_recv):
    row = lax.axis_index("row")
    feat = lax.axis_index("feat")
    z = row // X
    x = lax.rem(row, X)
    chunk_width = chunks[0].shape[1]
    width = STEP
    sub = width // 128

    def fetch(c):
        lanes = pl.ds(c * chunk_width, chunk_width)
        return pltpu.make_async_copy(codes_hbm.at[:, lanes], chunks[c], code_sem.at[c])

    small = [pltpu.make_async_copy(src, dst, small_sem.at[i]) for i, (src, dst) in enumerate(
        ((pairs_hbm, pairs_ref), (grad_hbm, grad_ref), (hess_hbm, hess_ref), (owners_hbm, owners_ref)))]
    fetch(0).start()
    for copy in small:
        copy.start()
    for c in range(1, CHUNKS):
        fetch(c).start()

    def z_peer(step):
        return (lax.rem(z + step, Z) * X + x, feat)

    def plane_peer(dx, df):
        return (z * X + lax.rem(x + dx, X), lax.rem(feat + df, FEAT))

    barrier = pltpu.get_barrier_semaphore()
    for step in Z_STEPS:
        pl.semaphore_signal(barrier, inc=1, device_id=z_peer(step), device_id_type=MESH)
    for dx, df in PLANE_STEPS:
        pl.semaphore_signal(barrier, inc=1, device_id=plane_peer(dx, df), device_id_type=MESH)

    level = lax.broadcasted_iota(jnp.int32, (16, width), 0).astype(jnp.float32).astype(jnp.bfloat16)
    level_up = level + jnp.bfloat16(16)
    one = jnp.ones((16, width), jnp.bfloat16)
    zero = jnp.zeros((16, width), jnp.bfloat16)

    def accumulate(c, codes, inner):
        start = inner * width
        block = c * (chunk_width // width) + inner

        def spread(ref):
            rows = ref[pl.ds(block * sub, sub), :].astype(jnp.float32)
            flat = jnp.concatenate([rows[j:j + 1, :] for j in range(sub)], axis=1)
            return jnp.broadcast_to(flat, (16, width)).astype(jnp.bfloat16)

        grad = spread(grad_ref)
        hess = spread(hess_ref)
        streamed, held = [], []
        for i in range(PAIRS):
            p = feat * PAIRS + i
            ca = codes[pl.ds(pairs_ref[0, p], 1), pl.ds(start, width)].astype(jnp.float32)
            cb = codes[pl.ds(pairs_ref[1, p], 1), pl.ds(start, width)].astype(jnp.float32)
            ca = jnp.broadcast_to(ca, (16, width)).astype(jnp.bfloat16)
            cb = jnp.broadcast_to(cb, (16, width)).astype(jnp.bfloat16)
            held += [jnp.where(cb <= level, one, zero), jnp.where(cb <= level_up, one, zero)]
            low, high = ca <= level, ca <= level_up
            streamed += [jnp.where(low, grad, zero), jnp.where(high, grad, zero),
                         jnp.where(low, hess, zero), jnp.where(high, hess, zero)]
        product = lax.dot_general(jnp.concatenate(streamed, axis=0), jnp.concatenate(held, axis=0),
                                  (((1,), (1,)), ((), ())), preferred_element_type=jnp.float32)
        for i in range(PAIRS):
            tile = product[64 * i:64 * i + 64, 128 * (i // 4):128 * (i // 4) + 128]
            acc[i] = tile if block == 0 else acc[i] + tile

    for copy in small:
        copy.wait()
    for c in range(CHUNKS):
        fetch(c).wait()
        for inner in range(chunk_width // width):
            accumulate(c, chunks[c], inner)

    lane = lax.broadcasted_iota(jnp.int32, (BINS, 128), 1)
    for i in range(X):
        both_pairs = [jnp.where(lax.rem(lane, 64) < 32, acc[2 * i, k:k + 32], acc[2 * i + 1, k:k + 32])
                      for k in (0, 32)]
        away = 1 - i % 2
        both_pairs[away] = pltpu.roll(both_pairs[away], 64, 1)
        send[i] = jnp.where(lane < 64, both_pairs[0], both_pairs[1])

    pl.semaphore_wait(barrier, Z - 1 + X * FEAT - 1)

    for dx in (2, 1, 3):
        other = lax.rem(x + dx, X)
        pltpu.make_async_remote_copy(
            src_ref=send.at[other], dst_ref=recv.at[x], send_sem=x_send, recv_sem=x_recv,
            device_id=(z * X + other, feat), device_id_type=MESH).start()

    mine = owners_ref[...] == feat
    mine_value = jnp.where(mine, 1.0, 0.0).astype(jnp.bfloat16)
    before = lax.broadcasted_iota(jnp.int32, (64, 64), 0) < lax.broadcasted_iota(jnp.int32, (64, 64), 1)
    rank = jnp.dot(mine_value, jnp.where(before, 1.0, 0.0).astype(jnp.bfloat16),
                   preferred_element_type=jnp.float32)
    slot = lax.broadcasted_iota(jnp.int32, (16, 64), 0).astype(jnp.float32)
    chosen = jnp.where((jnp.broadcast_to(rank, (16, 64)) == slot) & jnp.broadcast_to(mine, (16, 64)),
                       1.0, 0.0).astype(jnp.bfloat16)
    pair = lax.broadcasted_iota(jnp.int32, (64, 64), 0)
    place = lax.broadcasted_iota(jnp.int32, (64, 64), 1)
    order = jnp.where(pair == 2 * lax.rem(place, 32) + place // 32, 1.0, 0.0).astype(jnp.bfloat16)
    chosen = jnp.dot(chosen, order, preferred_element_type=jnp.float32)

    recv[x] = send[x]
    others = recv.at[pl.ds(0, X - 1)]
    pltpu.make_async_copy(others, others, x_recv).wait()
    parts[z] = jnp.sum(recv[...], axis=0)

    for step in Z_STEPS:
        pltpu.make_async_remote_copy(
            src_ref=parts.at[z], dst_ref=parts.at[z], send_sem=z_send, recv_sem=z_recv,
            device_id=z_peer(step), device_id_type=MESH).start()
    others = parts.at[pl.ds(0, Z - 1)]
    pltpu.make_async_copy(others, others, z_recv).wait()
    total = jnp.sum(parts[...], axis=0)

    def ends(values):
        return jnp.where(lane < 32, jnp.broadcast_to(values[:, 31:32], (BINS, 128)),
                         jnp.broadcast_to(values[:, 63:64], (BINS, 128)))

    grad_cum = total
    hess_cum = pltpu.roll(total, 64, 1)
    grad_end = ends(grad_cum)
    hess_end = ends(hess_cum)
    grad_col = grad_cum[31:32]
    hess_col = hess_cum[31:32]
    grad_all = grad_end[31:32]
    hess_all = hess_end[31:32]
    quad_grad = (grad_cum, grad_end - grad_cum, grad_col - grad_cum, grad_all - grad_end - grad_col + grad_cum)
    quad_hess = (hess_cum, hess_end - hess_cum, hess_col - hess_cum, hess_all - hess_end - hess_col + hess_cum)
    valid = lane < 64
    gain = -(grad_all * grad_all) / (hess_all + LAMBDA_REG)
    for grad_part, hess_part in zip(quad_grad, quad_hess):
        safe = jnp.where(valid, hess_part, 0.0)
        gain = gain + grad_part * grad_part / (safe + LAMBDA_REG)
    gain_ref[...] = gain.reshape(Z, X, 128)
    top = jnp.max(gain, axis=0, keepdims=True)
    lane_row = lane[0:1]
    lowest = jnp.float32(-jnp.inf)
    top_left = jnp.max(jnp.where(lane_row < 32, top, lowest), axis=1, keepdims=True)
    top_right = jnp.max(jnp.where((lane_row >= 32) & (lane_row < 64), top, lowest), axis=1, keepdims=True)
    pair_lane = 64 + feat * PAIRS + 2 * x
    peaks = jnp.where(lane_row == pair_lane, top_left, jnp.where(lane_row == pair_lane + 1, top_right, 0.0))
    own = jnp.where(lane[0:X] < 64, gain_ref[z], peaks)
    message[...] = own.reshape(X, 1, 128)

    here = feat * X + x
    for dx, df in PLANE_STEPS:
        pltpu.make_async_remote_copy(
            src_ref=message.at[lax.rem(x + dx, X)], dst_ref=inbox.at[here],
            send_sem=plane_send, recv_sem=plane_recv,
            device_id=plane_peer(dx, df), device_id_type=MESH).start()
    inbox[here] = message[x]
    others = inbox.at[pl.ds(0, X * FEAT - 1)]
    pltpu.make_async_copy(others, others, plane_recv).wait()
    news = inbox[...].reshape(X * FEAT, 128)
    table_ref[...] = jnp.dot(chosen, jnp.concatenate([news[:, 0:32], news[:, 32:64]], axis=0),
                             precision=lax.Precision.HIGHEST, preferred_element_type=jnp.float32)
    best = jnp.sum(news, axis=0, keepdims=True)
    best_ref[...] = best[:, 64:128]

    sent = recv.at[pl.ds(0, X - 1)]
    pltpu.make_async_copy(sent, sent, x_send).wait()
    sent = parts.at[pl.ds(0, Z - 1)]
    pltpu.make_async_copy(sent, sent, z_send).wait()
    sent = inbox.at[pl.ds(0, X * FEAT - 1)]
    pltpu.make_async_copy(sent, sent, plane_send).wait()


def shards(bin_codes, gradients, hessians, pair_list, owners):
    rows = bin_codes.shape[1]
    anywhere = pl.BlockSpec(memory_space=pl.ANY)
    vmem = pl.BlockSpec(memory_space=pltpu.VMEM)
    table, best = pl.pallas_call(
        kernel,
        out_shape=(pltpu.VMEM((16, BINS), jnp.float32), pltpu.VMEM((1, FEAT * PAIRS), jnp.float32)),
        in_specs=[anywhere] * 5,
        out_specs=(vmem, vmem),
        scratch_shapes=[[pltpu.VMEM((bin_codes.shape[0], rows // CHUNKS), jnp.int32)] * CHUNKS,
            pltpu.SMEM((2, FEAT * PAIRS), jnp.int32),
            pltpu.VMEM((1, FEAT * PAIRS), jnp.int32),
            pltpu.VMEM((rows // 128, 128), jnp.bfloat16),
            pltpu.VMEM((rows // 128, 128), jnp.bfloat16),
            pltpu.VMEM((PAIRS, 64, 128), jnp.float32),
            pltpu.VMEM((X, BINS, 128), jnp.float32),
            pltpu.VMEM((X, BINS, 128), jnp.float32),
            pltpu.VMEM((Z, BINS, 128), jnp.float32),
            pltpu.VMEM((Z, X, 128), jnp.float32),
            pltpu.VMEM((X, 1, 128), jnp.float32),
            pltpu.VMEM((X * FEAT, 1, 128), jnp.float32),
            pltpu.SemaphoreType.DMA((CHUNKS,)),
            pltpu.SemaphoreType.DMA((4,)),
        ] + [pltpu.SemaphoreType.DMA] * 6,
        compiler_params=pltpu.CompilerParams(collective_id=0, has_side_effects=True),
    )(pair_list.T, owners.reshape(1, -1), gradients.reshape(rows // 128, 128),
      hessians.reshape(rows // 128, 128), bin_codes)
    return table, best.reshape(-1)


def solution(mesh):
    in_specs = (P(None, "row"), P("row"), P("row"), P(), P())
    out_specs = (P("feat", "row"), P())
    return jax.shard_map(shards, mesh=mesh, in_specs=in_specs, out_specs=out_specs, check_vma=False)
```

```python
import jax
import jax.numpy as jnp
from jax import lax
from jax.experimental import pallas as pl
from jax.experimental.pallas import tpu as pltpu
from jax.sharding import PartitionSpec as P

BINS = 32
LAMBDA_REG = 1.0
Z = 8
X = 4
FEAT = 8
PAIRS = 8
CHUNKS = (1024, 3072, 4096)
STEP = 1024
MESH = pl.DeviceIdType.MESH
Z_STEPS = (4, 3, 5, 2, 6, 1, 7)
PLANE_STEPS = sorted(
    [(dx, df) for dx in range(X) for df in range(FEAT) if (dx, df) != (0, 0)],
    key=lambda s: -(min(s[0], X - s[0]) + min(s[1], FEAT - s[1]) / 2),
)


def kernel(pairs_hbm, owners_hbm, grad_hbm, hess_hbm, codes_hbm, table_ref, best_ref,
           chunks, pairs_ref, owners_ref, grad_ref, hess_ref,
           acc, send, recv, parts, gain_ref, message, inbox,
           code_sem, small_sem, x_send, x_recv, z_send, z_recv, plane_send, plane_recv):
    row = lax.axis_index("row")
    feat = lax.axis_index("feat")
    z = row // X
    x = lax.rem(row, X)
    width = STEP
    sub = width // 128

    def fetch(c):
        lanes = pl.ds(sum(CHUNKS[:c]), CHUNKS[c])
        return pltpu.make_async_copy(codes_hbm.at[:, lanes], chunks[c], code_sem.at[c])

    small = [pltpu.make_async_copy(src, dst, small_sem.at[i]) for i, (src, dst) in enumerate(
        ((pairs_hbm, pairs_ref), (grad_hbm, grad_ref), (hess_hbm, hess_ref), (owners_hbm, owners_ref)))]
    fetch(0).start()
    for copy in small:
        copy.start()
    for c in range(1, len(CHUNKS)):
        fetch(c).start()

    def z_peer(step):
        return (lax.rem(z + step, Z) * X + x, feat)

    def plane_peer(dx, df):
        return (z * X + lax.rem(x + dx, X), lax.rem(feat + df, FEAT))

    barrier = pltpu.get_barrier_semaphore()
    for step in Z_STEPS:
        pl.semaphore_signal(barrier, inc=1, device_id=z_peer(step), device_id_type=MESH)
    for dx, df in PLANE_STEPS:
        pl.semaphore_signal(barrier, inc=1, device_id=plane_peer(dx, df), device_id_type=MESH)

    level = lax.broadcasted_iota(jnp.int32, (16, width), 0).astype(jnp.float32).astype(jnp.bfloat16)
    level_up = level + jnp.bfloat16(16)
    one = jnp.ones((16, width), jnp.bfloat16)
    zero = jnp.zeros((16, width), jnp.bfloat16)

    def accumulate(c, codes, inner):
        start = inner * width
        block = sum(CHUNKS[:c]) // width + inner

        def spread(ref):
            rows = ref[pl.ds(block * sub, sub), :].astype(jnp.float32)
            flat = jnp.concatenate([rows[j:j + 1, :] for j in range(sub)], axis=1)
            return jnp.broadcast_to(flat, (16, width)).astype(jnp.bfloat16)

        grad = spread(grad_ref)
        hess = spread(hess_ref)
        for group in range(2):
            first, second = [], []
            for i in range(4):
                p = feat * PAIRS + group * 4 + i
                ca = codes[pl.ds(pairs_ref[0, p], 1), pl.ds(start, width)].astype(jnp.float32)
                cb = codes[pl.ds(pairs_ref[1, p], 1), pl.ds(start, width)].astype(jnp.float32)
                ca = jnp.broadcast_to(ca, (16, width)).astype(jnp.bfloat16)
                cb = jnp.broadcast_to(cb, (16, width)).astype(jnp.bfloat16)
                first += [jnp.where(ca <= level, one, zero), jnp.where(ca <= level_up, one, zero)]
                low, high = cb <= level, cb <= level_up
                second.append([[jnp.where(low, w, zero), jnp.where(high, w, zero)] for w in (grad, hess)])
            columns = [tile for i in (0, 2) for w in range(2) for j in (i, i + 1) for tile in second[j][w]]
            product = lax.dot_general(jnp.concatenate(first, axis=0), jnp.concatenate(columns, axis=0),
                                      (((1,), (1,)), ((), ())), preferred_element_type=jnp.float32)
            for half in range(2):
                tile = product[64 * half:64 * half + 64, 128 * half:128 * half + 128]
                k = 2 * group + half
                acc[k] = tile if block == 0 else acc[k] + tile

    for copy in small:
        copy.wait()
    for c in range(len(CHUNKS)):
        fetch(c).wait()
        for inner in range(CHUNKS[c] // width):
            accumulate(c, chunks[c], inner)

    lane = lax.broadcasted_iota(jnp.int32, (BINS, 128), 1)
    for i in range(X):
        send[i] = jnp.where(lax.rem(lane, 64) < 32, acc[i, 0:32], acc[i, 32:64])

    pl.semaphore_wait(barrier, Z - 1 + X * FEAT - 1)

    for dx in (2, 1, 3):
        other = lax.rem(x + dx, X)
        pltpu.make_async_remote_copy(
            src_ref=send.at[other], dst_ref=recv.at[x], send_sem=x_send, recv_sem=x_recv,
            device_id=(z * X + other, feat), device_id_type=MESH).start()

    mine = owners_ref[...] == feat
    mine_value = jnp.where(mine, 1.0, 0.0).astype(jnp.bfloat16)
    before = lax.broadcasted_iota(jnp.int32, (64, 64), 0) < lax.broadcasted_iota(jnp.int32, (64, 64), 1)
    rank = jnp.dot(mine_value, jnp.where(before, 1.0, 0.0).astype(jnp.bfloat16),
                   preferred_element_type=jnp.float32)
    slot = lax.broadcasted_iota(jnp.int32, (16, 64), 0).astype(jnp.float32)
    chosen = jnp.where((jnp.broadcast_to(rank, (16, 64)) == slot) & jnp.broadcast_to(mine, (16, 64)),
                       1.0, 0.0).astype(jnp.bfloat16)
    pair = lax.broadcasted_iota(jnp.int32, (64, 64), 0)
    place = lax.broadcasted_iota(jnp.int32, (64, 64), 1)
    order = jnp.where(pair == 2 * lax.rem(place, 32) + place // 32, 1.0, 0.0).astype(jnp.bfloat16)
    chosen = jnp.dot(chosen, order, preferred_element_type=jnp.float32)

    recv[x] = send[x]
    others = recv.at[pl.ds(0, X - 1)]
    pltpu.make_async_copy(others, others, x_recv).wait()
    parts[z] = jnp.sum(recv[...], axis=0)

    for step in Z_STEPS:
        pltpu.make_async_remote_copy(
            src_ref=parts.at[z], dst_ref=parts.at[z], send_sem=z_send, recv_sem=z_recv,
            device_id=z_peer(step), device_id_type=MESH).start()
    others = parts.at[pl.ds(0, Z - 1)]
    pltpu.make_async_copy(others, others, z_recv).wait()
    total = jnp.sum(parts[...], axis=0)

    def ends(values):
        return jnp.where(lane < 32, jnp.broadcast_to(values[:, 31:32], (BINS, 128)),
                         jnp.broadcast_to(values[:, 63:64], (BINS, 128)))

    grad_cum = total
    hess_cum = pltpu.roll(total, 64, 1)
    grad_end = ends(grad_cum)
    hess_end = ends(hess_cum)
    grad_col = grad_cum[31:32]
    hess_col = hess_cum[31:32]
    grad_all = grad_end[31:32]
    hess_all = hess_end[31:32]
    quad_grad = (grad_cum, grad_end - grad_cum, grad_col - grad_cum, grad_all - grad_end - grad_col + grad_cum)
    quad_hess = (hess_cum, hess_end - hess_cum, hess_col - hess_cum, hess_all - hess_end - hess_col + hess_cum)
    valid = lane < 64
    gain = -(grad_all * grad_all) / (hess_all + LAMBDA_REG)
    for grad_part, hess_part in zip(quad_grad, quad_hess):
        safe = jnp.where(valid, hess_part, 0.0)
        gain = gain + grad_part * grad_part / (safe + LAMBDA_REG)
    gain_ref[...] = gain.reshape(Z, X, 128)
    top = jnp.max(gain, axis=0, keepdims=True)
    lane_row = lane[0:1]
    lowest = jnp.float32(-jnp.inf)
    top_left = jnp.max(jnp.where(lane_row < 32, top, lowest), axis=1, keepdims=True)
    top_right = jnp.max(jnp.where((lane_row >= 32) & (lane_row < 64), top, lowest), axis=1, keepdims=True)
    pair_lane = 64 + feat * PAIRS + 2 * x
    peaks = jnp.where(lane_row == pair_lane, top_left, jnp.where(lane_row == pair_lane + 1, top_right, 0.0))
    own = jnp.where(lane[0:X] < 64, gain_ref[z], peaks)
    message[...] = own.reshape(X, 1, 128)

    here = feat * X + x
    for dx, df in PLANE_STEPS:
        pltpu.make_async_remote_copy(
            src_ref=message.at[lax.rem(x + dx, X)], dst_ref=inbox.at[here],
            send_sem=plane_send, recv_sem=plane_recv,
            device_id=plane_peer(dx, df), device_id_type=MESH).start()
    inbox[here] = message[x]
    others = inbox.at[pl.ds(0, X * FEAT - 1)]
    pltpu.make_async_copy(others, others, plane_recv).wait()
    news = inbox[...].reshape(X * FEAT, 128)
    table_ref[...] = jnp.dot(chosen, jnp.concatenate([news[:, 0:32], news[:, 32:64]], axis=0),
                             precision=lax.Precision.HIGHEST, preferred_element_type=jnp.float32)
    best = jnp.sum(news, axis=0, keepdims=True)
    best_ref[...] = best[:, 64:128]

    sent = recv.at[pl.ds(0, X - 1)]
    pltpu.make_async_copy(sent, sent, x_send).wait()
    sent = parts.at[pl.ds(0, Z - 1)]
    pltpu.make_async_copy(sent, sent, z_send).wait()
    sent = inbox.at[pl.ds(0, X * FEAT - 1)]
    pltpu.make_async_copy(sent, sent, plane_send).wait()


def shards(bin_codes, gradients, hessians, pair_list, owners):
    rows = bin_codes.shape[1]
    anywhere = pl.BlockSpec(memory_space=pl.ANY)
    vmem = pl.BlockSpec(memory_space=pltpu.VMEM)
    table, best = pl.pallas_call(
        kernel,
        out_shape=(pltpu.VMEM((16, BINS), jnp.float32), pltpu.VMEM((1, FEAT * PAIRS), jnp.float32)),
        in_specs=[anywhere] * 5,
        out_specs=(vmem, vmem),
        scratch_shapes=[[pltpu.VMEM((bin_codes.shape[0], c), jnp.int32) for c in CHUNKS],
            pltpu.SMEM((2, FEAT * PAIRS), jnp.int32),
            pltpu.VMEM((1, FEAT * PAIRS), jnp.int32),
            pltpu.VMEM((rows // 128, 128), jnp.bfloat16),
            pltpu.VMEM((rows // 128, 128), jnp.bfloat16),
            pltpu.VMEM((X, 64, 128), jnp.float32),
            pltpu.VMEM((X, BINS, 128), jnp.float32),
            pltpu.VMEM((X, BINS, 128), jnp.float32),
            pltpu.VMEM((Z, BINS, 128), jnp.float32),
            pltpu.VMEM((Z, X, 128), jnp.float32),
            pltpu.VMEM((X, 1, 128), jnp.float32),
            pltpu.VMEM((X * FEAT, 1, 128), jnp.float32),
            pltpu.SemaphoreType.DMA((len(CHUNKS),)),
            pltpu.SemaphoreType.DMA((4,)),
        ] + [pltpu.SemaphoreType.DMA] * 6,
        compiler_params=pltpu.CompilerParams(collective_id=0, has_side_effects=True),
    )(pair_list.T, owners.reshape(1, -1), gradients.reshape(rows // 128, 128),
      hessians.reshape(rows // 128, 128), bin_codes)
    return table, best.reshape(-1)


def solution(mesh):
    in_specs = (P(None, "row"), P("row"), P("row"), P(), P())
    out_specs = (P("feat", "row"), P())
    return jax.shard_map(shards, mesh=mesh, in_specs=in_specs, out_specs=out_specs, check_vma=False)
```
